32 devices in a mesh: dp: 8 (over z, x), tensor: 4 (over y, core).
Axes of the slice: x: 2, y: 2, z: 4, core: 2. Of those that a mesh axis runs over, the one named last changes fastest.
Arguments:
- layer_input: bfloat16 [16384, 768], P('dp'), may hold values from -6 to 6
- memory: bfloat16 [8192, 768], P('dp'), may hold values from -6 to 6
- cotangent: bfloat16 [16384, 768], P(('dp', 'tensor')), may hold values from -6 to 6
- seq_len: int32 [16], P('dp'), may hold values from 256 to 1024, as said below
- mem_len: int32 [16], P('dp'), may hold values from 128 to 512, as said below
- w_self_in: bfloat16 [3, 768, 768], P(None, None, 'tensor'), may hold values from -0.21875 to 0.21875
- b_self_in: float32 [2, 768], P(None, 'tensor'), may hold values from -3 to 3
- w_self_out: bfloat16 [768, 768], P('tensor'), may hold values from -0.875 to 0.875
- b_self_out: float32 [768], replicated, may hold values from -2 to 2
- w_cross_in: bfloat16 [3, 768, 768], P(None, None, 'tensor'), may hold values from -0.21875 to 0.21875
- b_cross_in: float32 [2, 768], P(None, 'tensor'), may hold values from -3 to 3
- w_cross_out: bfloat16 [768, 768], P('tensor'), may hold values from -0.875 to 0.875
- b_cross_out: float32 [768], replicated, may hold values from -2 to 2
- w_up: bfloat16 [768, 3072], P(None, 'tensor'), may hold values from -0.21875 to 0.21875
- b_up: float32 [3072], P('tensor'), may hold values from -3 to 3
- w_down: bfloat16 [3072, 768], P('tensor'), may hold values from -0.15625 to 0.15625
- b_down: float32 [768], replicated, may hold values from -2 to 2
- norm_gain: float32 [3, 768], replicated, may hold values from 0.5 to 1.5
- norm_bias: float32 [3, 768], replicated, may hold values from -2 to 2
Outputs:
- layer_output: bfloat16 [16384, 768], P(('dp', 'tensor'))
- input_grad: bfloat16 [16384, 768], P(('dp', 'tensor'))
- memory_grad: bfloat16 [8192, 768], P(('dp', 'tensor'))
- g_w_self_in: float32 [3, 768, 768], P(None, None, 'tensor')
- g_b_self_in: float32 [2, 768], P(None, 'tensor')
- g_w_self_out: float32 [768, 768], P('tensor')
- g_b_self_out: float32 [768], replicated
- g_w_cross_in: float32 [3, 768, 768], P(None, None, 'tensor')
- g_b_cross_in: float32 [2, 768], P(None, 'tensor')
- g_w_cross_out: float32 [768, 768], P('tensor')
- g_b_cross_out: float32 [768], replicated
- g_w_up: float32 [768, 3072], P(None, 'tensor')
- g_b_up: float32 [3072], P('tensor')
- g_w_down: float32 [3072, 768], P('tensor')
- g_b_down: float32 [768], replicated
- g_norm_gain: float32 [3, 768], replicated
- g_norm_bias: float32 [3, 768], replicated
- root_means: float32 [4], replicated
The draws below stay inside these ranges and needn't reach their ends.
Inputs may be any that keep to these rules, and one draw needn't show every extreme that they name: `seq_len`: A sequence's valid tokens are its first ones; some sequence has 1024 and some has 256. `mem_len`: A sequence's valid memory slots are its first ones; some sequence has 512 and some has 128.
All inputs are finite; a program needn't handle non-finite values.
Results may differ from the reference program's by a relative error of at most 0.03.
Values may be sent and summed in bfloat16 or wider, within the bound.
No kernel may reach another device: no remote copies, remote signals or barrier semaphores. Data moves between devices by JAX's collectives and lax.ppermute only.
A program may use at most 192 MiB of HBM per device.

```python
import jax
import jax.numpy as jnp
from jax import lax

D = 768
HEADS = 12
HD = 64
FF = 3072
LEN = 1024
MEM = 512
SEQUENCES = 16
TOKENS = 16384
MEM_ROWS = 8192


def draw_seq_len(key, part):
    lengths = jax.random.randint(jax.random.fold_in(key, 11), (SEQUENCES,), LEN // 4, LEN + 1, dtype=jnp.int32)
    return lengths.at[0].set(LEN).at[SEQUENCES - 1].set(LEN // 4)


def draw_mem_len(key, part):
    lengths = jax.random.randint(jax.random.fold_in(key, 23), (SEQUENCES,), MEM // 4, MEM + 1, dtype=jnp.int32)
    return lengths.at[1].set(MEM).at[SEQUENCES - 2].set(MEM // 4)


def levels(key, dims, shards, least, largest):
    def one(dim, shards_of):
        heights = jax.random.uniform(jax.random.fold_in(jax.random.fold_in(key, 6), dim), (shards_of,), jnp.float32, least / len(shards), largest / len(shards))
        return jnp.repeat(jnp.exp(heights), dims[dim] // shards_of).reshape((-1,) + (1,) * (len(dims) - dim - 1))

    factor_of = one(*shards[0])
    for cut in shards[1:]:
        factor_of = factor_of * one(*cut)
    return factor_of


def bell_draw(key, shape, spread, reach, cuts=(), kind=jnp.bfloat16):
    array = spread * jax.random.normal(key, shape, jnp.float32)
    if cuts:
        array = array * levels(key, shape, cuts, -0.22, 0.18)
    return jnp.clip(array, -reach, reach).astype(kind)


def setup_inputs(seed: int = 0) -> dict:
    key_list = jax.random.split(jax.random.key(seed), 20)
    return {
        "layer_input": bell_draw(key_list[0], (TOKENS, D), 1.0, 6.0, ((0, 8),)),
        "memory": bell_draw(key_list[1], (MEM_ROWS, D), 1.0, 6.0, ((0, 8),)),
        "cotangent": bell_draw(key_list[2], (TOKENS, D), 1.0, 6.0, ((0, 32),)),
        "seq_len": draw_seq_len(jax.random.fold_in(key_list[19], 71), 0),
        "mem_len": draw_mem_len(jax.random.fold_in(key_list[19], 71), 0),
        "w_self_in": bell_draw(key_list[5], (3, D, D), D ** -0.5, 0.21875, ((2, 4),)),
        "b_self_in": bell_draw(key_list[6], (2, D), 0.5, 3.0, ((1, 4),), jnp.float32),
        "w_self_out": bell_draw(key_list[7], (D, D), (D // 16) ** -0.5, 0.875, ((0, 4),)),
        "b_self_out": bell_draw(key_list[8], (D,), 0.3, 2.0, (), jnp.float32),
        "w_cross_in": bell_draw(key_list[9], (3, D, D), D ** -0.5, 0.21875, ((2, 4),)),
        "b_cross_in": bell_draw(key_list[10], (2, D), 0.5, 3.0, ((1, 4),), jnp.float32),
        "w_cross_out": bell_draw(key_list[11], (D, D), (D // 16) ** -0.5, 0.875, ((0, 4),)),
        "b_cross_out": bell_draw(key_list[12], (D,), 0.3, 2.0, (), jnp.float32),
        "w_up": bell_draw(key_list[13], (D, FF), D ** -0.5, 0.21875, ((1, 4),)),
        "b_up": bell_draw(key_list[14], (FF,), 0.5, 3.0, ((0, 4),), jnp.float32),
        "w_down": bell_draw(key_list[15], (FF, D), (FF // 2) ** -0.5, 0.15625, ((0, 4),)),
        "b_down": bell_draw(key_list[16], (D,), 0.3, 2.0, (), jnp.float32),
        "norm_gain": jnp.clip(1.0 + 0.1 * jax.random.normal(key_list[17], (3, D), jnp.float32), 0.5, 1.5),
        "norm_bias": bell_draw(key_list[18], (3, D), 0.3, 2.0, (), jnp.float32),
    }


@jax.custom_vjp
def low(v):
    return lax.optimization_barrier(v.astype(jnp.bfloat16)).astype(jnp.float32)

@jax.custom_vjp
def low_back(v):
    return v

def low_keep(v):
    return (low(v), None)

def low_pass(kept, grad):
    return (grad,)

def back_keep(v):
    return (v, None)

def back_low(kept, grad):
    return (low(grad),)
low.defvjp(low_keep, low_pass)
low_back.defvjp(back_keep, back_low)

def matmul(left, right):
    return jnp.dot(left, right, precision=lax.Precision.HIGHEST, preferred_element_type=jnp.float32)

def normalize(values, gain, shift):
    row_mean = lax.optimization_barrier(jnp.mean(values, axis=-1, keepdims=True))
    centered = values - row_mean
    variance = lax.optimization_barrier(jnp.mean(centered * centered, axis=-1, keepdims=True))
    return centered * lax.rsqrt(variance + 1e-05) * gain + shift

def attend(query_in, key_in, w_in, b_in, w_out, b_out, allowed):
    query_count = query_in.shape[0]
    key_count = key_in.shape[0]
    queries = low_back(low(matmul(query_in, w_in[0]) + b_in[0])).reshape(query_count, HEADS, HD)
    key_rows = low_back(low(matmul(key_in, w_in[1]))).reshape(key_count, HEADS, HD)
    value_rows = low_back(low(matmul(key_in, w_in[2]) + b_in[1])).reshape(key_count, HEADS, HD)
    scores = jnp.einsum('qhd,khd->hqk', queries, key_rows, precision=lax.Precision.HIGHEST) * HD ** (-0.5)
    scores = low_back(jnp.where(allowed[None], scores, -1e+30))
    probs = jax.nn.softmax(scores, axis=-1)
    mixed = jnp.einsum('hqk,khd->qhd', low(probs), value_rows, precision=lax.Precision.HIGHEST)
    mixed = low_back(low(mixed.reshape(query_count, HEADS * HD)))
    return low_back(matmul(mixed, w_out) + b_out)

def layer(params, inputs, memory_rows, length, mem_length):
    w_self_in, b_self_in, w_self_out, b_self_out, w_cross_in, b_cross_in, w_cross_out, b_cross_out, w_up, b_up, w_down, b_down, norm_gain, norm_bias = params
    positions = jnp.arange(LEN)
    mem_positions = jnp.arange(MEM)
    self_allowed = (positions[None, :] <= positions[:, None]) & (positions[None, :] < length)
    cross_allowed = jnp.broadcast_to(mem_positions[None, :] < mem_length, (LEN, MEM))
    input_low = low(inputs)
    self_out = attend(input_low, input_low, w_self_in, b_self_in, w_self_out, b_self_out, self_allowed)
    first_norm = normalize(inputs + self_out, norm_gain[0], norm_bias[0])
    cross_out = attend(low(first_norm), low(memory_rows), w_cross_in, b_cross_in, w_cross_out, b_cross_out, cross_allowed)
    second_norm = normalize(first_norm + cross_out, norm_gain[1], norm_bias[1])
    hidden = low_back(matmul(low(second_norm), w_up) + b_up)
    ffn_out = low_back(matmul(low(jax.nn.gelu(hidden, approximate=False)), w_down) + b_down)
    result = normalize(second_norm + ffn_out, norm_gain[2], norm_bias[2])
    valid = (positions < length).astype(inputs.dtype)[:, None]
    squares = jnp.stack([jnp.sum(valid * inputs * inputs), jnp.sum(valid * self_out * self_out), jnp.sum(valid * cross_out * cross_out), jnp.sum(valid * ffn_out * ffn_out)])
    return (result, squares)

def reference(layer_input, memory, cotangent, seq_len, mem_len, w_self_in, b_self_in, w_self_out, b_self_out, w_cross_in, b_cross_in, w_cross_out, b_cross_out, w_up, b_up, w_down, b_down, norm_gain, norm_bias):
    params = (w_self_in.astype(jnp.float32), b_self_in.astype(jnp.float32), w_self_out.astype(jnp.float32), b_self_out.astype(jnp.float32), w_cross_in.astype(jnp.float32), b_cross_in.astype(jnp.float32), w_cross_out.astype(jnp.float32), b_cross_out.astype(jnp.float32), w_up.astype(jnp.float32), b_up.astype(jnp.float32), w_down.astype(jnp.float32), b_down.astype(jnp.float32), norm_gain.astype(jnp.float32), norm_bias.astype(jnp.float32))
    inputs_all = layer_input.astype(jnp.float32).reshape(SEQUENCES, LEN, D)
    memory_all = memory.astype(jnp.float32).reshape(SEQUENCES, MEM, D)
    checked = jax.checkpoint(layer)

    def forward(weights, inputs_in, memory_in):

        def step(carry, packed):
            result, squares = checked(weights, packed[0], packed[1], packed[2], packed[3])
            return (carry, (result, squares))
        unused, (results, squares) = lax.scan(step, jnp.zeros((), jnp.float32), (inputs_in, memory_in, seq_len, mem_len))
        return (results, squares)
    results, pullback, squares = jax.vjp(forward, params, inputs_all, memory_all, has_aux=True)
    valid = (jnp.arange(LEN)[None, :] < seq_len[:, None]).astype(jnp.float32)
    seed_grad = cotangent.astype(jnp.float32).reshape(SEQUENCES, LEN, D) * valid[:, :, None]
    weight_grads, input_grad, memory_grad = pullback(seed_grad)
    root_means = jnp.sqrt(lax.optimization_barrier(jnp.sum(squares, axis=0)) / (jnp.sum(valid) * D))
    return (results.reshape(TOKENS, D).astype(jnp.bfloat16), input_grad.reshape(TOKENS, D).astype(jnp.bfloat16), memory_grad.reshape(MEM_ROWS, D).astype(jnp.bfloat16), weight_grads[0], weight_grads[1], weight_grads[2], weight_grads[3], weight_grads[4], weight_grads[5], weight_grads[6], weight_grads[7], weight_grads[8], weight_grads[9], weight_grads[10], weight_grads[11], weight_grads[12], weight_grads[13], root_means)
```

```python
import jax
import jax.numpy as jnp
from jax import lax
from jax.sharding import PartitionSpec as P

HD = 64
BF = jnp.bfloat16
F32 = jnp.float32


def project(inputs, weight):
    return jnp.dot(inputs, weight, preferred_element_type=F32)


def outer_sum(left, right):
    return lax.dot_general(left, right, (((0,), (0,)), ((), ())), preferred_element_type=F32)


def times_transposed(left, right):
    return lax.dot_general(left, right, (((1,), (1,)), ((), ())), preferred_element_type=F32)


def swap(values, axis, bit):
    size = lax.axis_size(axis)
    return lax.ppermute(values, axis, [(i, i ^ bit) for i in range(size)])


def gelu_exact(values):
    return jax.nn.gelu(values, approximate=False)


def allowed_keys(offset, block_rows, key_count, key_limit, causal):
    key_index = jnp.arange(key_count, dtype=jnp.int32)[None, :]
    kept_keys = key_index < key_limit
    if causal:
        query_index = offset + jnp.arange(block_rows, dtype=jnp.int32)[:, None]
        kept_keys = kept_keys & (key_index <= query_index)
    return jnp.broadcast_to(kept_keys, (block_rows, key_count))


def heads_of(values):
    return values.reshape(values.shape[0], -1, HD)


def attend_forward(queries, keys, values, key_limit, causal):
    query_rows, key_rows, value_rows = heads_of(queries), heads_of(keys), heads_of(values)
    block_rows = min(512, queries.shape[0])
    score_scale = HD ** (-0.5)
    mixed_parts = []
    log_parts = []
    for offset in range(0, query_rows.shape[0], block_rows):
        key_count = min(key_rows.shape[0], offset + block_rows) if causal else key_rows.shape[0]
        kept_keys = allowed_keys(offset, block_rows, key_count, key_limit, causal)
        scores = (
            jnp.einsum(
                "qhd,khd->hqk",
                query_rows[offset : offset + block_rows],
                key_rows[:key_count],
                preferred_element_type=F32,
            )
            * score_scale
        )
        scores = jnp.where(kept_keys[None], scores, -1e30)
        row_max = jnp.max(scores, axis=-1, keepdims=True)
        exponent = jnp.exp(scores - row_max)
        row_sum = jnp.sum(exponent, axis=-1, keepdims=True)
        weights = (exponent / row_sum).astype(BF)
        mixed_parts.append(
            jnp.einsum(
                "hqk,khd->qhd", weights, value_rows[:key_count], preferred_element_type=F32
            ).astype(BF)
        )
        log_parts.append((row_max + jnp.log(row_sum))[..., 0])
    mixed = jnp.concatenate(mixed_parts, axis=0)
    return mixed.reshape(queries.shape), jnp.concatenate(log_parts, axis=1)


def attend_backward(queries, keys, values, logs, grads, key_limit, causal):
    query_rows, key_rows, value_rows = heads_of(queries), heads_of(keys), heads_of(values)
    grad_rows = heads_of(grads)
    block_rows = min(512, queries.shape[0])
    score_scale = HD ** (-0.5)
    grad_keys = jnp.zeros(key_rows.shape, F32)
    grad_values = jnp.zeros(value_rows.shape, F32)
    query_parts = []
    for offset in range(0, query_rows.shape[0], block_rows):
        key_count = min(key_rows.shape[0], offset + block_rows) if causal else key_rows.shape[0]
        query_block = query_rows[offset : offset + block_rows]
        grad_block = grad_rows[offset : offset + block_rows]
        kept_keys = allowed_keys(offset, block_rows, key_count, key_limit, causal)
        scores = (
            jnp.einsum(
                "qhd,khd->hqk", query_block, key_rows[:key_count], preferred_element_type=F32
            )
            * score_scale
        )
        scores = jnp.where(kept_keys[None], scores, -1e30)
        probs = jnp.exp(scores - logs[:, offset : offset + block_rows, None])
        grad_probs = jnp.einsum(
            "qhd,khd->hqk", grad_block, value_rows[:key_count], preferred_element_type=F32
        )
        inner_sum = jnp.sum(probs * grad_probs, axis=-1, keepdims=True)
        grad_scores = (probs * (grad_probs - inner_sum)).astype(BF)
        query_parts.append(
            jnp.einsum(
                "hqk,khd->qhd", grad_scores, key_rows[:key_count], preferred_element_type=F32
            )
            * score_scale
        )
        block_keys = (
            jnp.einsum("hqk,qhd->khd", grad_scores, query_block, preferred_element_type=F32)
            * score_scale
        )
        block_values = jnp.einsum(
            "hqk,qhd->khd", probs.astype(BF), grad_block, preferred_element_type=F32
        )
        grad_keys = grad_keys.at[:key_count].add(block_keys)
        grad_values = grad_values.at[:key_count].add(block_values)
    grad_queries = jnp.concatenate(query_parts, axis=0)
    return (
        grad_queries.astype(BF).reshape(queries.shape),
        grad_keys.astype(BF).reshape(keys.shape),
        grad_values.astype(BF).reshape(values.shape),
    )


def normalize(combined):
    row_mean = jnp.mean(combined, axis=-1, keepdims=True)
    centered = combined - row_mean
    variance = jnp.mean(centered * centered, axis=-1, keepdims=True)
    inverse_scale = lax.rsqrt(variance + 1e-05)
    return centered * inverse_scale, inverse_scale


def norm_back(upstream, unit_rows, inverse_scale, gain):
    scaled = upstream * gain
    result_grad = inverse_scale * (
        scaled
        - jnp.mean(scaled, axis=-1, keepdims=True)
        - unit_rows * jnp.mean(scaled * unit_rows, axis=-1, keepdims=True)
    )
    return (result_grad, jnp.sum(upstream * unit_rows, axis=0), jnp.sum(upstream, axis=0))


def half_pick(values, bit, axis=0):
    half = values.shape[axis] // 2
    return lax.dynamic_slice_in_dim(values, bit * half, half, axis)


def dp_sum(part):
    size = lax.axis_size("dp")
    place = lax.axis_index("dp")
    bits = []
    bit = 1
    while bit < size:
        bits.append(bit)
        bit *= 2
    for bit in bits:
        mine = (place // bit) % 2
        away = half_pick(part, 1 - mine).astype(BF)
        kept = half_pick(part, mine)
        part = kept.astype(F32) + swap(away, "dp", bit).astype(F32)
    part = part.astype(BF)
    for bit in bits[::-1]:
        mine = (place // bit) % 2
        other = swap(part, "dp", bit)
        part = jnp.where(
            mine == 0, jnp.concatenate([part, other]), jnp.concatenate([other, part])
        )
    return part.astype(F32)


def grad_sum(own, other):
    return dp_sum(own + swap(other.astype(BF), "tensor", 2).astype(F32))


def everywhere_sum(packed):
    for axis in ("tensor", "dp"):
        bit = 1
        while bit < lax.axis_size(axis):
            packed = packed + swap(packed, axis, bit)
            bit *= 2
    return packed


def pack(arrays):
    flat = jnp.concatenate([a.reshape(-1) for a in arrays])
    room = -flat.shape[0] % 1024
    return jnp.pad(flat, (0, room)).reshape(-1, 128)


def unpack(packed, shapes):
    flat = packed.reshape(-1)
    out = []
    start = 0
    for shape in shapes:
        count = 1
        for dim in shape:
            count *= dim
        out.append(flat[start : start + count].reshape(shape))
        start += count
    return out


def shards(
    layer_input,
    memory,
    cotangent,
    seq_len,
    mem_len,
    w_self_in,
    b_self_in,
    w_self_out,
    b_self_out,
    w_cross_in,
    b_cross_in,
    w_cross_out,
    b_cross_out,
    w_up,
    b_up,
    w_down,
    b_down,
    norm_gain,
    norm_bias,
):
    ways = lax.axis_size("tensor")
    sequence_count = seq_len.shape[0]
    assert ways == 2 * sequence_count
    model_width = layer_input.shape[1]
    seq_length = layer_input.shape[0] // sequence_count
    mem_length = memory.shape[0] // sequence_count
    share_rows = seq_length // 2
    place = lax.axis_index("tensor")
    pair = place // 2
    core = place % 2
    head_cols = w_self_in.shape[2]
    my_len = lax.dynamic_slice_in_dim(seq_len, pair, 1, 0)[0]
    my_mem_len = lax.dynamic_slice_in_dim(mem_len, pair, 1, 0)[0]
    x = lax.dynamic_slice_in_dim(layer_input, pair * seq_length, seq_length, 0)
    mem = lax.dynamic_slice_in_dim(memory, pair * mem_length, mem_length, 0)
    x_mine = half_pick(x, core).astype(F32)
    row_index = core * share_rows + jnp.arange(share_rows, dtype=jnp.int32)
    valid_mine = (row_index < my_len).astype(F32)

    def both(own, axis):
        return jnp.concatenate([own, swap(own, "tensor", 2)], axis=axis)

    def side_by_side(weights):
        return jnp.concatenate([weights[0], weights[1], weights[2]], axis=1)

    def three(joined):
        own, other = joined
        cut = lambda a, i: a[..., i * head_cols : (i + 1) * head_cols]
        return [jnp.concatenate([cut(own, i), cut(other, i)], axis=-1) for i in range(3)]

    own_self = side_by_side(w_self_in)
    other_self = swap(own_self, "tensor", 2)
    w_q1, w_k1, w_v1 = three((own_self, other_self))
    biases = jnp.concatenate([b_self_in, b_cross_in, b_up.reshape(-1, head_cols)], axis=0)
    biases_other = swap(biases, "tensor", 2)
    b_join = lambda i: jnp.concatenate([biases[i], biases_other[i]])
    b_up_join = jnp.concatenate([b_up, biases_other[4:].reshape(-1)])
    w_so = both(w_self_out, 0)
    own_cross = side_by_side(w_cross_in)
    other_cross = swap(own_cross, "tensor", 2)
    w_q2, w_k2, w_v2 = three((own_cross, other_cross))
    w_co = both(w_cross_out, 0)
    w_up2 = both(w_up, 1)
    w_down2 = both(w_down, 0)

    def pair_sum(away, mine, kind):
        return mine + swap(away.astype(kind), "tensor", 1).astype(F32)

    def halves(values):
        return half_pick(values, core), half_pick(values, 1 - core)

    def pair_rows(own):
        return jnp.concatenate([own, swap(own, "tensor", 1)], axis=0)

    q1 = (project(x, w_q1) + b_join(0)).astype(BF)
    k1 = project(x, w_k1).astype(BF)
    v1 = (project(x, w_v1) + b_join(1)).astype(BF)
    o1, logs1 = attend_forward(q1, k1, v1, my_len, True)
    k2 = project(mem, w_k2).astype(BF)
    v2 = (project(mem, w_v2) + b_join(3)).astype(BF)

    def square_of(branch):
        return jnp.sum(valid_mine[:, None] * branch * branch)

    def post_norm(rows_mine, rows_away, weight, bias, residual, index):
        away = project(rows_away, weight)
        branch = pair_sum(away, project(rows_mine, weight), BF) + bias
        unit, scale = normalize(residual + branch)
        return unit * norm_gain[index] + norm_bias[index], unit, scale, square_of(branch)

    h1, unit1, scale1, square1 = post_norm(*halves(o1), w_so, b_self_out, x_mine, 0)
    h1_rows = pair_rows(h1.astype(BF))
    q2 = (project(h1_rows, w_q2) + b_join(2)).astype(BF)
    o2, logs2 = attend_forward(q2, k2, v2, my_mem_len, False)
    h2, unit2, scale2, square2 = post_norm(
        o2[:share_rows], o2[share_rows:], w_co, b_cross_out, h1, 1
    )
    h2_rows = pair_rows(h2.astype(BF))
    hidden = project(h2_rows, w_up2) + b_up_join
    active = gelu_exact(hidden).astype(BF)
    out, unit3, scale3, square3 = post_norm(
        active[:share_rows], active[share_rows:], w_down2, b_down, h2, 2
    )

    dy = cotangent.astype(F32) * valid_mine[:, None]
    dr3, gain3, shift3 = norm_back(dy, unit3, scale3, norm_gain[2])
    dz = pair_rows(dr3.astype(BF))
    ff = w_down.shape[0]
    g_down = grad_sum(outer_sum(active[:, :ff], dz), outer_sum(active[:, ff:], dz))
    d_active = times_transposed(dz, w_down2)
    unused, pullback = jax.vjp(gelu_exact, hidden)
    du = pullback(d_active)[0].astype(BF)
    g_up = grad_sum(outer_sum(h2_rows, du[:, :ff]), outer_sum(h2_rows, du[:, ff:]))
    dh2 = dr3 + pair_sum(
        times_transposed(du[share_rows:], w_up2), times_transposed(du[:share_rows], w_up2), BF
    )
    dr2, gain2, shift2 = norm_back(dh2, unit2, scale2, norm_gain[1])
    dc = pair_rows(dr2.astype(BF))
    g_cross_out = grad_sum(
        outer_sum(o2[:, :head_cols], dc), outer_sum(o2[:, head_cols:], dc)
    )
    do2 = times_transposed(dc, w_co).astype(BF)
    dq2, dk2, dv2 = attend_backward(q2, k2, v2, logs2, do2, my_mem_len, False)

    def in_grads(rows_q, rows_kv, dq, dk, dv):
        def one(cols):
            return jnp.concatenate(
                [
                    outer_sum(rows_q, dq[:, cols]),
                    outer_sum(rows_kv, dk[:, cols]),
                    outer_sum(rows_kv, dv[:, cols]),
                ],
                axis=1,
            )

        total = grad_sum(one(slice(0, head_cols)), one(slice(head_cols, 2 * head_cols)))
        return jnp.stack([total[:, i * head_cols : (i + 1) * head_cols] for i in range(3)])

    g_cross_in = in_grads(h1_rows, mem, dq2, dk2, dv2)
    dh1 = (
        dr2
        + pair_sum(
            times_transposed(dq2[share_rows:], w_q2), times_transposed(dq2[:share_rows], w_q2), BF
        )
    )

    def back_kv(index):
        return times_transposed(half_pick(dk2, index), w_k2) + times_transposed(
            half_pick(dv2, index), w_v2
        )

    memory_grad = pair_sum(back_kv(1 - core), back_kv(core), BF).astype(BF)
    dr1, gain1, shift1 = norm_back(dh1, unit1, scale1, norm_gain[0])
    da_mine = dr1.astype(BF)
    da_peer = swap(da_mine, "tensor", 1)
    da = jnp.where(
        core == 0, jnp.concatenate([da_mine, da_peer]), jnp.concatenate([da_peer, da_mine])
    )
    g_self_out = grad_sum(outer_sum(o1[:, :head_cols], da), outer_sum(o1[:, head_cols:], da))
    do1 = times_transposed(da, w_so).astype(BF)
    dq1, dk1, dv1 = attend_backward(q1, k1, v1, logs1, do1, my_len, True)
    g_self_in = in_grads(x, x, dq1, dk1, dv1)

    def back_self(index):
        return (
            times_transposed(half_pick(dq1, index), w_q1)
            + times_transposed(half_pick(dk1, index), w_k1)
            + times_transposed(half_pick(dv1, index), w_v1)
        )

    input_grad = (dr1 + pair_sum(back_self(1 - core), back_self(core), BF)).astype(BF)

    slot = (jnp.arange(ways) == core).astype(F32)[:, None]
    slot_other = (jnp.arange(ways) == core + 2).astype(F32)[:, None]
    own_slot = jnp.where(pair == 0, slot, slot_other)
    other_slot = jnp.where(pair == 0, slot_other, slot)

    def slots(row):
        count = row.shape[0] // 2
        return own_slot * row[None, :count] + other_slot * row[None, count:]

    def column_sum(values):
        return jnp.sum(values.astype(F32), axis=0)

    squares = jnp.stack([square_of(x_mine), square1, square2, square3, jnp.sum(valid_mine)])
    early = [
        jnp.pad(squares, (0, 123)),
        gain2,
        gain3,
        shift2,
        shift3,
        column_sum(dr3.astype(BF)),
        column_sum(dr2.astype(BF)),
        slots(column_sum(du)),
        slots(column_sum(dq2)),
        slots(column_sum(dv2)),
    ]
    late = [
        gain1,
        shift1,
        column_sum(da_mine),
        slots(column_sum(dq1)),
        slots(column_sum(dv1)),
    ]
    early_sum = unpack(everywhere_sum(pack(early)), [a.shape for a in early])
    late_sum = unpack(everywhere_sum(pack(late)), [a.shape for a in late])

    def mine_of(rows):
        return lax.dynamic_slice_in_dim(rows, place, 1, 0)[0]

    square_total = early_sum[0][:4]
    valid_total = early_sum[0][4]
    return (
        out.astype(BF),
        input_grad,
        memory_grad,
        g_self_in,
        jnp.stack([mine_of(late_sum[3]), mine_of(late_sum[4])]),
        g_self_out,
        late_sum[2],
        g_cross_in,
        jnp.stack([mine_of(early_sum[8]), mine_of(early_sum[9])]),
        g_cross_out,
        early_sum[6],
        g_up,
        mine_of(early_sum[7]),
        g_down,
        early_sum[5],
        jnp.stack([late_sum[0], early_sum[1], early_sum[2]]),
        jnp.stack([late_sum[1], early_sum[3], early_sum[4]]),
        jnp.sqrt(square_total / (valid_total * model_width)),
    )


def solution(mesh):
    in_specs = (
        P("dp", None),
        P("dp", None),
        P(("dp", "tensor"), None),
        P("dp"),
        P("dp"),
        P(None, None, "tensor"),
        P(None, "tensor"),
        P("tensor", None),
        P(),
        P(None, None, "tensor"),
        P(None, "tensor"),
        P("tensor", None),
        P(),
        P(None, "tensor"),
        P("tensor"),
        P("tensor", None),
        P(),
        P(),
        P(),
    )
    out_specs = (
        P(("dp", "tensor"), None),
        P(("dp", "tensor"), None),
        P(("dp", "tensor"), None),
        P(None, None, "tensor"),
        P(None, "tensor"),
        P("tensor", None),
        P(),
        P(None, None, "tensor"),
        P(None, "tensor"),
        P("tensor", None),
        P(),
        P(None, "tensor"),
        P("tensor"),
        P("tensor", None),
        P(),
        P(),
        P(),
        P(),
    )
    return jax.shard_map(shards, mesh=mesh, in_specs=in_specs, out_specs=out_specs, check_vma=False)
```
